128 devices in a mesh: layer: 16 (over z, y_lo, core), lat: 8 (over x, y_hi).
Axes of the slice: x: 4, y: 4 (y_hi: 2, y_lo: 2; y = y_hi * 2 + y_lo), z: 4, core: 2. Of those that a mesh axis runs over, the one named last changes fastest.
Arguments:
- green: bfloat16 [16, 2, 2, 128, 4, 2, 128, 128], P('layer', None, None, 'lat'), may hold values from -0.15625 to 0.15625
- block_index: int32 [16, 2, 128, 4], P('layer', None, 'lat'), may hold values from 0 to 127
- sources: float32 [16, 2, 2, 2, 16384], P('layer', None, None, None, 'lat'), may hold values from -6 to 6
Outputs:
- down_traces: float32 [16, 2, 2, 16384], P('layer', None, None, 'lat')
- up_traces: float32 [16, 2, 2, 16384], P('layer', None, None, 'lat')
The draws below stay inside these ranges and needn't reach their ends.
Inputs may be any that keep to these rules, and one draw needn't show every extreme that they name: `block_index`: block numbers of the whole trace, which has 128 blocks; repeats within a block row may occur.
All inputs are finite; a program needn't handle non-finite values.
Results may differ from the reference program's by a relative error of at most 0.013.
Values may be sent and summed in bfloat16 or wider, within the bound.
No kernel may reach another device: no remote copies, remote signals or barrier semaphores. Data moves between devices by JAX's collectives and lax.ppermute only.
A program may use at most 128 MiB of HBM per device.

```python
import jax
import jax.numpy as jnp
from jax import lax

NF = 2
BSIZE = 128
K = 4
LAYERS = 16
BLOCKS = 128
TRACE = 16384


def place_ends(drawn, stream_key, low, largest):
    place = [jax.random.randint(jax.random.fold_in(stream_key, axis), (), 0, length) for axis, length in enumerate(drawn.shape)]
    widest = drawn.shape.index(max(drawn.shape))
    next_to = place[:widest] + [(place[widest] + 1) % drawn.shape[widest]] + place[widest + 1:]
    return drawn.at[tuple(place)].set(low).at[tuple(next_to)].set(largest)


def level_of(rng, extent, split, least, top_value):
    factor_of, own = 1.0, jax.random.fold_in(rng, 6)
    for axis_at, shards_of in split:
        steps = jnp.exp(jax.random.uniform(jax.random.fold_in(own, axis_at), (shards_of,), jnp.float32, least / len(split), top_value / len(split)))
        factor_of = factor_of * jnp.repeat(steps, extent[axis_at] // shards_of).reshape([-1 if axis == axis_at else 1 for axis in range(len(extent))])
    return factor_of


def centred(key, extent, deviation, reach, shards=(), kind=jnp.bfloat16):
    values = jax.random.normal(key, extent, jnp.float32) * deviation
    if len(shards) > 0:
        values = level_of(key, extent, shards, -0.22, 0.18) * values
    return jnp.clip(values, min=-reach, max=reach).astype(kind)


def setup_inputs(seed: int = 0) -> dict:
    arg_keys = jax.random.split(jax.random.key(seed), 4)
    green = centred(arg_keys[0], (LAYERS, 2, NF, BLOCKS, K, 2, BSIZE, BSIZE), (5 * K * BSIZE // 2) ** -0.5, 0.15625, ((0, 16), (3, 8)))
    block_index = place_ends(jax.random.randint(arg_keys[1], (LAYERS, 2, BLOCKS, K), 0, BLOCKS), jax.random.fold_in(arg_keys[1], 1), 0, BLOCKS - 1).astype(jnp.int32)
    sources = centred(arg_keys[2], (LAYERS, 2, 2, NF, TRACE), 1.0, 6.0, ((0, 16), (4, 8)), jnp.float32)
    return {"green": green, "block_index": block_index, "sources": sources}


def layer_apply(green_layer, index_layer, trace_low):
    pieces = trace_low.reshape(2, NF, BLOCKS, BSIZE)[:, :, index_layer].astype(jnp.float32)
    real_mat = green_layer[:, :, :, 0].astype(jnp.float32)
    imag_mat = green_layer[:, :, :, 1].astype(jnp.float32)
    real_out = jnp.einsum('fbkij,fbkj->fbi', real_mat, pieces[0]) - jnp.einsum('fbkij,fbkj->fbi', imag_mat, pieces[1])
    imag_out = jnp.einsum('fbkij,fbkj->fbi', real_mat, pieces[1]) + jnp.einsum('fbkij,fbkj->fbi', imag_mat, pieces[0])
    return jnp.stack([real_out, imag_out]).reshape(2, NF, TRACE)


def reference(green, block_index, sources):
    def down_step(carry, layer_id):
        result = layer_apply(green[layer_id, 0], block_index[layer_id, 0], carry) + sources[layer_id, 0]
        return result.astype(jnp.bfloat16), result

    def up_step(carry, layer_id):
        result = layer_apply(green[layer_id, 1], block_index[layer_id, 1], carry) + sources[layer_id, 1]
        return result.astype(jnp.bfloat16), result

    start = jnp.zeros((2, NF, TRACE), jnp.bfloat16)
    layer_ids = jnp.arange(LAYERS).astype(jnp.int32)
    _, down_traces = lax.scan(down_step, start, layer_ids)
    _, up_traces = lax.scan(up_step, start, layer_ids, reverse=True)
    return down_traces, up_traces
```

```python
import functools
import itertools

import jax
import jax.numpy as jnp
from jax import lax
from jax.experimental import pallas as pl
from jax.experimental.pallas import tpu as pltpu
from jax.sharding import PartitionSpec as P


LAYERS = 16
LAT = 8
AXES = ("layer", "lat")
BF = jnp.bfloat16
F32 = jnp.float32


def successors():
    plan, late = [], set()
    for t in range(LAYERS - 1):
        s, r, s2, r2 = t, t + 1, LAYERS - 1 - t, LAYERS - 2 - t
        if s == r2:
            succ, now_late = {s: r, r: s}, set()
            rest = [l for l in range(LAYERS) if l not in (s, r)]
        else:
            avail = [l for l in range(LAYERS) if l not in (s, r, s2, r2)]

            def cost(l):
                return 10 * (l in late) + 10 * (l in (t + 2, LAYERS - 3 - t))

            best = None
            for q, p, q2, p2 in itertools.permutations(avail, 4):
                c = 3 * cost(q) + cost(p) + 3 * cost(q2) + cost(p2)
                c += 0.1 * (abs(r - q) + abs(q - p) + abs(p - s) + abs(r2 - q2) + abs(q2 - p2) + abs(p2 - s2))
                left = [l for l in avail if l not in (q, p, q2, p2)]
                c += 0.3 * sum((l ^ 1) not in left for l in left)
                if best is None or c < best[0]:
                    best = (c, q, p, q2, p2)
            _, q, p, q2, p2 = best
            succ = {s: r, r: q, q: p, p: s, s2: r2, r2: q2, q2: p2, p2: s2}
            rest = [l for l in avail if l not in (q, p, q2, p2)]
            now_late = {q, p, q2, p2, s, s2}
        single = [l for l in rest if (l ^ 1) not in rest]
        succ.update({l: l ^ 1 for l in rest if (l ^ 1) in rest})
        succ.update({l: single[(i + 1) % len(single)] for i, l in enumerate(single)})
        plan.append(succ)
        late = now_late
    return plan


def shift_pairs(succ, t, flip):
    live = {(t, t + 1), (LAYERS - 1 - t, LAYERS - 2 - t)}
    return sorted(
        (a * LAT + j, b * LAT + ((j ^ flip) if (a, b) in live else j))
        for a, b in succ.items()
        for j in range(LAT)
    )


def load_kernel(green_ref, out_ref, sem):
    copy = pltpu.make_async_copy(green_ref, out_ref, sem)
    copy.start()
    copy.wait()


def load(green):
    return pl.pallas_call(
        load_kernel,
        out_shape=pltpu.VMEM(green.shape, green.dtype),
        in_specs=[pl.BlockSpec(memory_space=pl.ANY)],
        out_specs=pl.BlockSpec(memory_space=pltpu.VMEM),
        scratch_shapes=[pltpu.SemaphoreType.DMA],
        compiler_params=pltpu.CompilerParams(vmem_limit_bytes=2**20),
        name="load_green",
    )(green)


def apply_kernel(t, layer_ref, sel_ref, src_ref, green_ref, *refs):
    layer = layer_ref[0]

    @pl.when((layer == t) | (layer == LAYERS - 1 - t))
    def _():
        active_kernel((layer != t).astype(jnp.int32), sel_ref, src_ref, green_ref, *refs)


def active_kernel(way, sel_ref, src_ref, green_ref, *refs):
    *trace_refs, _, outs_ref, piece_ref = refs
    nf, nb, nk = green_ref.shape[1:4]
    sel = sel_ref[way]
    picked = []
    for c in range(2):
        row = []
        for f in range(nf):
            at = (c * nf + f) * nb
            parts = []
            for ref in trace_refs:
                for p in range(ref.shape[0] // (2 * nf * nb)):
                    parts.append(ref[p * 2 * nf * nb + at : p * 2 * nf * nb + at + nb, :])
            x = jnp.concatenate(parts, axis=0)
            row.append(jnp.dot(sel, x, preferred_element_type=F32).astype(BF))
        picked.append(row)
    rows = lax.broadcasted_iota(jnp.int32, (2 * nb, 128), 0) % nb
    for f in range(nf):
        left = []
        for k in range(nk):
            p = picked[0][f][k * nb : (k + 1) * nb]
            q = picked[1][f][k * nb : (k + 1) * nb]
            left.append(jnp.concatenate([p, q], axis=0))
            left.append(jnp.concatenate([-q, p], axis=0))
        left = jnp.concatenate(left, axis=1)
        acc = jnp.zeros((2 * nb, 128), F32)
        for b in range(0, nb, 2):
            mats = []
            for i in range(2):
                mats.append(jnp.concatenate([green_ref[way, f, b + i, k, c] for k in range(nk) for c in range(2)], axis=1))
            out = lax.dot_general(left, jnp.concatenate(mats, axis=0), (((1,), (1,)), ((), ())), preferred_element_type=F32)
            acc = jnp.where(rows == b, out[:, :128], jnp.where(rows == b + 1, out[:, 128:], acc))
        for c in range(2):
            at = (c * nf + f) * nb
            y = acc[c * nb : (c + 1) * nb] + src_ref[way, at : at + nb, :]
            outs_ref[way, at : at + nb, :] = y
            piece_ref[at : at + nb, :] = y.astype(BF)


def apply(t, layer, sel, src, green, traces, outs):
    vmem = pl.BlockSpec(memory_space=pltpu.VMEM)
    return pl.pallas_call(
        functools.partial(apply_kernel, t),
        out_shape=(jax.ShapeDtypeStruct(outs.shape, F32), jax.ShapeDtypeStruct(outs.shape[1:], BF)),
        in_specs=[pl.BlockSpec(memory_space=pltpu.SMEM)] + [vmem] * (4 + len(traces)),
        out_specs=(vmem, vmem),
        input_output_aliases={4 + len(traces): 0},
        compiler_params=pltpu.CompilerParams(vmem_limit_bytes=8 * 2**20),
        name="apply_green",
    )(layer, sel, src, pltpu.with_memory_space_constraint(green, pltpu.VMEM), *traces, outs)


def local(green, block_index, sources):
    nf, nb, nk = green.shape[2:5]
    rows = 2 * nf * nb
    layer, lat = lax.axis_index("layer"), lax.axis_index("lat")
    green = load(green.reshape(green.shape[1:]))
    src = sources.reshape(2, rows, 128)
    sender = block_index[0] // nb
    place = (((lat // 2 - sender // 2) % 4) * 2 + (sender % 2 + lat % 2) % 2) * nb + block_index[0] % nb
    place = jnp.swapaxes(place, 1, 2).reshape(2, nk * nb, 1)
    sel = (place == jnp.arange(LAT * nb).reshape(1, 1, -1)).astype(BF)
    plan = successors()
    me = layer.astype(jnp.int32).reshape(1)

    def active(t):
        return (layer == t) | (layer == LAYERS - 1 - t)

    def turns(pair):
        turn = {k: lax.ppermute(pair, "lat", [(j, (j + 2 * k) % LAT) for j in range(LAT)]) for k in (2, 1, 3)}
        return pair, turn[1], turn[2], turn[3]

    outs = jnp.zeros((2, rows, 128), F32)
    zeros = jnp.zeros((2 * rows, 128), BF)
    outs, piece = apply(0, me, sel, src, green, (zeros,) * 4, outs)
    for t in range(LAYERS - 1):
        got = [lax.ppermute(piece, AXES, shift_pairs(plan[t], t, flip)) for flip in (1, 0)]
        pair = jnp.concatenate(got[::-1], axis=0)
        traces = lax.cond(active(t + 1), turns, lambda pair: (pair,) * 4, pair)
        outs, piece = apply(t + 1, me, sel, src, green, traces, outs)
    return outs[0].reshape(1, 2, nf, nb * 128), outs[1].reshape(1, 2, nf, nb * 128)


def solution(mesh):
    placed = (
        P("layer", None, None, "lat", None, None, None, None),
        P("layer", None, "lat", None),
        P("layer", None, None, None, "lat"),
    )
    return jax.shard_map(
        local,
        mesh=mesh,
        in_specs=placed,
        out_specs=(P("layer", None, None, "lat"), P("layer", None, None, "lat")),
        check_vma=False,
    )
```

```python
import functools
import itertools

import jax
import jax.numpy as jnp
from jax import lax
from jax.experimental import pallas as pl
from jax.experimental.pallas import tpu as pltpu
from jax.sharding import PartitionSpec as P


LAYERS = 16
LAT = 8
AXES = ("layer", "lat")
BF = jnp.bfloat16
F32 = jnp.float32


def successors():
    plan, late = [], set()
    for t in range(LAYERS - 1):
        s, r, s2, r2 = t, t + 1, LAYERS - 1 - t, LAYERS - 2 - t
        if s == r2:
            succ, now_late = {s: r, r: s}, set()
            rest = [l for l in range(LAYERS) if l not in (s, r)]
        else:
            avail = [l for l in range(LAYERS) if l not in (s, r, s2, r2)]

            def cost(l):
                return 10 * (l in late) + 10 * (l in (t + 2, LAYERS - 3 - t))

            best = None
            for q, p, q2, p2 in itertools.permutations(avail, 4):
                c = 3 * cost(q) + cost(p) + 3 * cost(q2) + cost(p2)
                c += 0.1 * (abs(r - q) + abs(q - p) + abs(p - s) + abs(r2 - q2) + abs(q2 - p2) + abs(p2 - s2))
                left = [l for l in avail if l not in (q, p, q2, p2)]
                c += 0.3 * sum((l ^ 1) not in left for l in left)
                if best is None or c < best[0]:
                    best = (c, q, p, q2, p2)
            _, q, p, q2, p2 = best
            succ = {s: r, r: q, q: p, p: s, s2: r2, r2: q2, q2: p2, p2: s2}
            rest = [l for l in avail if l not in (q, p, q2, p2)]
            now_late = {q, p, q2, p2, s, s2}
        single = [l for l in rest if (l ^ 1) not in rest]
        succ.update({l: l ^ 1 for l in rest if (l ^ 1) in rest})
        succ.update({l: single[(i + 1) % len(single)] for i, l in enumerate(single)})
        plan.append(succ)
        late = now_late
    return plan


def shift_pairs(succ, t, flip):
    live = {(t, t + 1), (LAYERS - 1 - t, LAYERS - 2 - t)}
    return sorted(
        (a * LAT + j, b * LAT + ((j ^ flip) if (a, b) in live else j))
        for a, b in succ.items()
        for j in range(LAT)
    )


def apply_kernel(t, layer_ref, sel_ref, src_ref, green_ref, *refs):
    layer = layer_ref[0]

    @pl.when((layer == t) | (layer == LAYERS - 1 - t))
    def _():
        active_kernel((layer != t).astype(jnp.int32), sel_ref, src_ref, green_ref, *refs)


def active_kernel(way, sel_ref, src_ref, green_ref, *refs):
    *trace_refs, _, outs_ref, piece_ref = refs
    nf, nb, nk = green_ref.shape[1:4]
    sel = sel_ref[way]
    rows = lax.broadcasted_iota(jnp.int32, (2 * nb, 128), 0) % nb

    def one(f, carry):
        picked = []
        for c in range(2):
            at = (c * nf + f) * nb
            parts = []
            for ref in trace_refs:
                for p in range(ref.shape[0] // (2 * nf * nb)):
                    parts.append(ref[pl.ds(pl.multiple_of(p * 2 * nf * nb + at, nb), nb), :])
            x = jnp.concatenate(parts, axis=0)
            picked.append(jnp.dot(sel, x, preferred_element_type=F32).astype(BF))
        left = []
        for k in range(nk):
            p = picked[0][k * nb : (k + 1) * nb]
            q = picked[1][k * nb : (k + 1) * nb]
            left.append(jnp.concatenate([p, q], axis=0))
            left.append(jnp.concatenate([-q, p], axis=0))
        left = jnp.concatenate(left, axis=1)
        acc = jnp.zeros((2 * nb, 128), F32)
        for b in range(0, nb, 2):
            mats = []
            for i in range(2):
                mats.append(jnp.concatenate([green_ref[way, f, b + i, k, c] for k in range(nk) for c in range(2)], axis=1))
            out = lax.dot_general(left, jnp.concatenate(mats, axis=0), (((1,), (1,)), ((), ())), preferred_element_type=F32)
            acc = jnp.where(rows == b, out[:, :128], jnp.where(rows == b + 1, out[:, 128:], acc))
        for c in range(2):
            at = pl.multiple_of((c * nf + f) * nb, nb)
            y = acc[c * nb : (c + 1) * nb] + src_ref[way, pl.ds(at, nb), :]
            outs_ref[way, pl.ds(at, nb), :] = y
            piece_ref[pl.ds(at, nb), :] = y.astype(BF)
        return carry

    lax.fori_loop(0, nf, one, 0)


def apply(t, layer, sel, src, green, traces, outs):
    vmem = pl.BlockSpec(memory_space=pltpu.VMEM)
    return pl.pallas_call(
        functools.partial(apply_kernel, t),
        out_shape=(jax.ShapeDtypeStruct(outs.shape, F32), jax.ShapeDtypeStruct(outs.shape[1:], BF)),
        in_specs=[pl.BlockSpec(memory_space=pltpu.SMEM)] + [vmem] * (4 + len(traces)),
        out_specs=(vmem, vmem),
        input_output_aliases={4 + len(traces): 0},
        compiler_params=pltpu.CompilerParams(vmem_limit_bytes=8 * 2**20),
        name="apply_green",
    )(layer, sel, src, green, *traces, outs)


def local(green, block_index, sources):
    nf, nb, nk = green.shape[2:5]
    rows = 2 * nf * nb
    layer, lat = lax.axis_index("layer"), lax.axis_index("lat")
    green = pltpu.with_memory_space_constraint(green.reshape(green.shape[1:]), pltpu.VMEM)
    src = sources.reshape(2, rows, 128)
    sender = block_index[0] // nb
    place = (((lat // 2 - sender // 2) % 4) * 2 + (sender % 2 + lat % 2) % 2) * nb + block_index[0] % nb
    place = jnp.swapaxes(place, 1, 2).reshape(2, nk * nb, 1)
    sel = (place == jnp.arange(LAT * nb).reshape(1, 1, -1)).astype(BF)
    plan = successors()
    me = layer.astype(jnp.int32).reshape(1)

    def turns(pair):
        turn = {k: lax.ppermute(pair, "lat", [(j, (j + 2 * k) % LAT) for j in range(LAT)]) for k in (2, 1, 3)}
        return pair, turn[1], turn[2], turn[3]

    outs = jnp.zeros((2, rows, 128), F32)
    zeros = jnp.zeros((2 * rows, 128), BF)
    outs, piece = apply(0, me, sel, src, green, (zeros,) * 4, outs)
    for t in range(LAYERS - 1):
        got = [lax.ppermute(piece, AXES, shift_pairs(plan[t], t, flip)) for flip in (1, 0)]
        pair = jnp.pad(got[1], ((0, rows), (0, 0))) + jnp.pad(got[0], ((rows, 0), (0, 0)))
        outs, piece = apply(t + 1, me, sel, src, green, turns(pair), outs)
    return outs[0].reshape(1, 2, nf, nb * 128), outs[1].reshape(1, 2, nf, nb * 128)


def solution(mesh):
    placed = (
        P("layer", None, None, "lat", None, None, None, None),
        P("layer", None, "lat", None),
        P("layer", None, None, None, "lat"),
    )
    return jax.shard_map(
        local,
        mesh=mesh,
        in_specs=placed,
        out_specs=(P("layer", None, None, "lat"), P("layer", None, None, "lat")),
        check_vma=False,
    )
```

```python
import functools
import itertools

import jax
import jax.numpy as jnp
from jax import lax
from jax.experimental import pallas as pl
from jax.experimental.pallas import tpu as pltpu
from jax.sharding import PartitionSpec as P


LAYERS = 16
LAT = 8
AXES = ("layer", "lat")
BF = jnp.bfloat16
F32 = jnp.float32


def successors():
    plan, late = [], set()
    for t in range(LAYERS - 1):
        s, r, s2, r2 = t, t + 1, LAYERS - 1 - t, LAYERS - 2 - t
        if s == r2:
            succ, now_late = {s: r, r: s}, set()
            rest = [l for l in range(LAYERS) if l not in (s, r)]
        else:
            avail = [l for l in range(LAYERS) if l not in (s, r, s2, r2)]

            def cost(l):
                return 10 * (l in late) + 10 * (l in (t + 2, LAYERS - 3 - t))

            best = None
            for q, p, q2, p2 in itertools.permutations(avail, 4):
                c = 3 * cost(q) + cost(p) + 3 * cost(q2) + cost(p2)
                c += 0.1 * (abs(r - q) + abs(q - p) + abs(p - s) + abs(r2 - q2) + abs(q2 - p2) + abs(p2 - s2))
                left = [l for l in avail if l not in (q, p, q2, p2)]
                c += 0.3 * sum((l ^ 1) not in left for l in left)
                if best is None or c < best[0]:
                    best = (c, q, p, q2, p2)
            _, q, p, q2, p2 = best
            succ = {s: r, r: q, q: p, p: s, s2: r2, r2: q2, q2: p2, p2: s2}
            rest = [l for l in avail if l not in (q, p, q2, p2)]
            now_late = {q, p, q2, p2, s, s2}
        single = [l for l in rest if (l ^ 1) not in rest]
        succ.update({l: l ^ 1 for l in rest if (l ^ 1) in rest})
        succ.update({l: single[(i + 1) % len(single)] for i, l in enumerate(single)})
        plan.append(succ)
        late = now_late
    return plan


def shift_pairs(succ, t, flip):
    live = {(t, t + 1), (LAYERS - 1 - t, LAYERS - 2 - t)}
    return sorted(
        (a * LAT + j, b * LAT + ((j ^ flip) if (a, b) in live else j))
        for a, b in succ.items()
        for j in range(LAT)
    )


def block_rows(c, f, nf, nb):
    return pl.ds(pl.multiple_of((c * nf + f) * nb, nb), nb)


def multiply(left_ref, way, sizes, weights, src_ref, outs_ref, piece_ref):
    nf, nb, nk = sizes
    half = nb // 2
    rows = lax.broadcasted_iota(jnp.int32, (nb, 128), 0) % half

    def one(f, carry):
        accs = []
        for h in range(2):
            left = left_ref[f, h]
            acc = jnp.zeros((nb, 128), F32)
            for b in range(0, half, 2):
                out = weights(left, f, h * half + b)
                acc = jnp.where(rows == b, out[:, :128], jnp.where(rows == b + 1, out[:, 128:], acc))
            accs.append(acc)
        for c in range(2):
            at = block_rows(c, f, nf, nb)
            y = jnp.concatenate([acc[c * half : (c + 1) * half] for acc in accs], axis=0) + src_ref[way, at, :]
            outs_ref[way, at, :] = y
            piece_ref[at, :] = y.astype(BF)
        return carry

    lax.fori_loop(0, nf, one, 0)


def first_kernel(layer_ref, sources_ref, green_ref, src_ref, outs_ref, piece_ref, raw_ref, mats_ref, left_ref, raw_sem, sems):
    nf, nb, nk = green_ref.shape[1:4]
    layer = layer_ref[0]
    way = (layer != 0).astype(jnp.int32)
    active = (layer == 0) | (layer == LAYERS - 1)
    raw_copy = pltpu.make_async_copy(sources_ref, raw_ref, raw_sem)
    raw_copy.start()

    def chunk(f, b):
        at = pl.ds(b, 2)
        return pltpu.make_async_copy(green_ref.at[way, f, at], mats_ref.at[f, at], sems.at[f, b // 2])

    @pl.when(active)
    def _():
        for f in range(nf):
            for b in range(0, nb, 2):
                chunk(f, b).start()

    raw_copy.wait()
    for w in range(2):
        for c in range(2):
            for f in range(nf):
                for b in range(nb):
                    at = (c * nf + f) * nb + b
                    src_ref[w, at : at + 1, :] = raw_ref[w, c, f : f + 1, b * 128 : (b + 1) * 128]

    @pl.when(active)
    def _():
        left_ref[...] = jnp.zeros_like(left_ref)

        def weights(left, f, b):
            chunk(f, b).wait()
            mats = [jnp.concatenate([mats_ref[f, b + i, k, c] for k in range(nk) for c in range(2)], axis=1) for i in range(2)]
            return lax.dot_general(left, jnp.concatenate(mats, axis=0), (((1,), (1,)), ((), ())), preferred_element_type=F32)

        multiply(left_ref, way, (nf, nb, nk), weights, src_ref, outs_ref, piece_ref)


def first(layer, sources, green):
    nf, nb, nk = green.shape[1:4]
    rows = 2 * nf * nb
    vmem, hbm = pl.BlockSpec(memory_space=pltpu.VMEM), pl.BlockSpec(memory_space=pltpu.HBM)
    return pl.pallas_call(
        first_kernel,
        out_shape=(
            jax.ShapeDtypeStruct((2, rows, 128), F32),
            jax.ShapeDtypeStruct((2, rows, 128), F32),
            jax.ShapeDtypeStruct((rows, 128), BF),
        ),
        in_specs=[pl.BlockSpec(memory_space=pltpu.SMEM), hbm, hbm],
        out_specs=(vmem, vmem, vmem),
        scratch_shapes=[
            pltpu.VMEM(sources.shape, F32),
            pltpu.VMEM(green.shape[1:], BF),
            pltpu.VMEM((nf, 2, nb, 2 * nk * 128), BF),
            pltpu.SemaphoreType.DMA,
            pltpu.SemaphoreType.DMA((nf, nb // 2)),
        ],
        compiler_params=pltpu.CompilerParams(vmem_limit_bytes=12 * 2**20),
        name="first_apply",
    )(layer, sources, green)


def turn_kernel(second, layer_ref, _, green_ref, *refs):
    turned_ref, stage_ref, sems = refs[-3:]
    nf, nb, nk = green_ref.shape[1:4]
    way = (layer_ref[0] >= LAYERS // 2).astype(jnp.int32)
    way = 1 - way if second else way
    slots, total = stage_ref.shape[0], nf * nb

    def fetch(i, slot):
        return pltpu.make_async_copy(green_ref.at[way, i // nb, i % nb], stage_ref.at[slot], sems.at[slot])

    for slot in range(slots):
        fetch(slot, slot).start()

    def some(n, carry):
        for slot in range(slots):
            i = n * slots + slot
            fetch(i, slot).wait()
            for k in range(nk):
                for c in range(2):
                    turned_ref[way, i // nb, i % nb, k, c] = stage_ref[slot, k, c].T

            @pl.when(i + slots < total)
            def _():
                fetch(i + slots, slot).start()

        return carry

    lax.fori_loop(0, total // slots, some, 0)


def turn(layer, after, green, turned=None):
    smem, vmem, hbm = (pl.BlockSpec(memory_space=m) for m in (pltpu.SMEM, pltpu.VMEM, pltpu.HBM))
    given = () if turned is None else (turned,)
    return pl.pallas_call(
        functools.partial(turn_kernel, turned is not None),
        out_shape=pltpu.VMEM(green.shape, BF),
        in_specs=[smem, vmem, hbm] + [vmem] * len(given),
        out_specs=vmem,
        scratch_shapes=[pltpu.VMEM((4, *green.shape[3:]), BF), pltpu.SemaphoreType.DMA((4,))],
        input_output_aliases={3: 0} if given else {},
        compiler_params=pltpu.CompilerParams(vmem_limit_bytes=2 * 2**20),
        cost_estimate=pl.CostEstimate(flops=0, bytes_accessed=16 * 2**20, transcendentals=0),
        name="turn_green",
    )(layer, after, green, *given)


def apply_kernel(t, layer_ref, sel_ref, src_ref, green_ref, *refs):
    *trace_refs, _, outs_ref, piece_ref, left_ref = refs
    layer = layer_ref[0]
    way = (layer != t).astype(jnp.int32)
    nf, nb, nk = green_ref.shape[1:4]
    part = 2 * nf * nb

    @pl.when((layer == t) | (layer == LAYERS - 1 - t))
    def _():
        columns = []
        for f in range(nf):
            rows = []
            for c in range(2):
                at = (c * nf + f) * nb
                for ref in trace_refs:
                    rows += [ref[p + at : p + at + nb, :] for p in range(0, ref.shape[0], part)]
            columns.append(jnp.concatenate(rows, axis=0))
        picked = jnp.dot(sel_ref[way], jnp.concatenate(columns, axis=1), preferred_element_type=F32).astype(BF)
        for f in range(nf):
            for h in range(2):
                blocks = [picked[(h * 2 * nk + n) * nb : (h * 2 * nk + n + 1) * nb, f * 128 : (f + 1) * 128] for n in range(2 * nk)]
                left_ref[f, h] = jnp.concatenate(blocks, axis=1)

        def weights(left, f, b):
            mats = [jnp.concatenate([green_ref[way, f, b + i, k, c] for k in range(nk) for c in range(2)], axis=0) for i in range(2)]
            return jnp.dot(left, jnp.concatenate(mats, axis=1), preferred_element_type=F32)

        multiply(left_ref, way, (nf, nb, nk), weights, src_ref, outs_ref, piece_ref)


def apply(t, layer, sel, src, green, traces, outs):
    nf, nb, nk = green.shape[1:4]
    vmem = pl.BlockSpec(memory_space=pltpu.VMEM)
    return pl.pallas_call(
        functools.partial(apply_kernel, t),
        out_shape=(jax.ShapeDtypeStruct(outs.shape, F32), jax.ShapeDtypeStruct(outs.shape[1:], BF)),
        in_specs=[pl.BlockSpec(memory_space=pltpu.SMEM)] + [vmem] * (4 + len(traces)),
        out_specs=(vmem, vmem),
        scratch_shapes=[pltpu.VMEM((nf, 2, nb, 2 * nk * 128), BF)],
        input_output_aliases={4 + len(traces): 0},
        compiler_params=pltpu.CompilerParams(vmem_limit_bytes=4 * 2**20),
        name="apply_green",
    )(layer, sel, src, green, *traces, outs)


def selection(index, lat, nb, nk):
    sender = index // nb
    place = (((lat // 2 - sender // 2) % 4) * 2 + (sender % 2 + lat % 2) % 2) * nb + index % nb
    place = place.reshape(2, 2, nb // 2, nk).transpose(0, 1, 3, 2)
    both = lax.broadcasted_iota(jnp.int32, (2, 2, nk, 2, 2, nb // 2), 3) != lax.broadcasted_iota(jnp.int32, (2, 2, nk, 2, 2, nb // 2), 4)
    minus = lax.broadcasted_iota(jnp.int32, (2, 2, nk, 2, 2, nb // 2), 3) > lax.broadcasted_iota(jnp.int32, (2, 2, nk, 2, 2, nb // 2), 4)
    column = place[:, :, :, None, None, :] + jnp.where(both, LAT * nb, 0)
    sign = jnp.where(minus, -1, 1)
    hit = column.reshape(2, -1, 1) == jnp.arange(2 * LAT * nb).reshape(1, 1, -1)
    return jnp.where(hit, sign.reshape(2, -1, 1), 0).astype(BF)


def local(green, block_index, sources):
    nf, nb, nk = green.shape[2:5]
    rows = 2 * nf * nb
    layer, lat = lax.axis_index("layer"), lax.axis_index("lat")
    me = layer.astype(jnp.int32).reshape(1)
    green = pltpu.with_memory_space_constraint(green.reshape(green.shape[1:]), pltpu.HBM)
    raw = pltpu.with_memory_space_constraint(sources.reshape(sources.shape[1:]), pltpu.HBM)
    src, outs, piece = first(me, raw, green)
    sel = selection(block_index[0], lat, nb, nk)
    plan = successors()
    turned = turn(me, piece, green)
    for t in range(LAYERS - 1):
        got = [lax.ppermute(piece, AXES, shift_pairs(plan[t], t, flip)) for flip in (1, 0)]
        pair = jnp.pad(got[1], ((0, rows), (0, 0))) + jnp.pad(got[0], ((rows, 0), (0, 0)))
        far = {k: lax.ppermute(pair, "lat", [(j, (j + 2 * k) % LAT) for j in range(LAT)]) for k in (2, 1, 3)}
        outs, piece = apply(t + 1, me, sel, src, turned, (pair, far[1], far[2], far[3]), outs)
        if t == 0:
            turned = turn(me, piece, green, turned)
    return outs[0].reshape(1, 2, nf, nb * 128), outs[1].reshape(1, 2, nf, nb * 128)


def solution(mesh):
    placed = (
        P("layer", None, None, "lat", None, None, None, None),
        P("layer", None, "lat", None),
        P("layer", None, None, None, "lat"),
    )
    return jax.shard_map(
        local,
        mesh=mesh,
        in_specs=placed,
        out_specs=(P("layer", None, None, "lat"), P("layer", None, None, "lat")),
        check_vma=False,
    )
```

```python
import functools
import itertools

import jax
import jax.numpy as jnp
from jax import lax
from jax.experimental import pallas as pl
from jax.experimental.pallas import tpu as pltpu
from jax.sharding import PartitionSpec as P


LAYERS = 16
LAT = 8
AXES = ("layer", "lat")
BF = jnp.bfloat16
F32 = jnp.float32


def successors():
    plan, late = [], set()
    for t in range(LAYERS - 1):
        s, r, s2, r2 = t, t + 1, LAYERS - 1 - t, LAYERS - 2 - t
        if s == r2:
            succ, now_late = {s: r, r: s}, set()
            rest = [l for l in range(LAYERS) if l not in (s, r)]
        else:
            avail = [l for l in range(LAYERS) if l not in (s, r, s2, r2)]

            def cost(l):
                return 10 * (l in late) + 10 * (l in (t + 2, LAYERS - 3 - t))

            best = None
            for q, p, q2, p2 in itertools.permutations(avail, 4):
                c = 3 * cost(q) + cost(p) + 3 * cost(q2) + cost(p2)
                c += 0.1 * (abs(r - q) + abs(q - p) + abs(p - s) + abs(r2 - q2) + abs(q2 - p2) + abs(p2 - s2))
                left = [l for l in avail if l not in (q, p, q2, p2)]
                c += 0.3 * sum((l ^ 1) not in left for l in left)
                if best is None or c < best[0]:
                    best = (c, q, p, q2, p2)
            _, q, p, q2, p2 = best
            succ = {s: r, r: q, q: p, p: s, s2: r2, r2: q2, q2: p2, p2: s2}
            rest = [l for l in avail if l not in (q, p, q2, p2)]
            now_late = {q, p, q2, p2, s, s2}
        single = [l for l in rest if (l ^ 1) not in rest]
        succ.update({l: l ^ 1 for l in rest if (l ^ 1) in rest})
        succ.update({l: single[(i + 1) % len(single)] for i, l in enumerate(single)})
        plan.append(succ)
        late = now_late
    return plan


def shift_pairs(succ, t, flip):
    live = {(t, t + 1), (LAYERS - 1 - t, LAYERS - 2 - t)}
    return sorted(
        (a * LAT + j, b * LAT + ((j ^ flip) if (a, b) in live else j))
        for a, b in succ.items()
        for j in range(LAT)
    )


def block_rows(c, f, nf, nb):
    return pl.ds(pl.multiple_of((c * nf + f) * nb, nb), nb)


def multiply(left_ref, way, sizes, weights, src_ref, outs_ref, piece_ref):
    nf, nb, nk = sizes
    half = nb // 2
    rows = lax.broadcasted_iota(jnp.int32, (nb, 128), 0) % half

    def one(f, carry):
        accs = []
        for h in range(2):
            left = left_ref[f, h]
            acc = jnp.zeros((nb, 128), F32)
            for b in range(0, half, 2):
                out = weights(left, f, h * half + b)
                acc = jnp.where(rows == b, out[:, :128], jnp.where(rows == b + 1, out[:, 128:], acc))
            accs.append(acc)
        for c in range(2):
            at = block_rows(c, f, nf, nb)
            y = jnp.concatenate([acc[c * half : (c + 1) * half] for acc in accs], axis=0) + src_ref[way, at, :]
            outs_ref[way, at, :] = y
            piece_ref[at, :] = y.astype(BF)
        return carry

    lax.fori_loop(0, nf, one, 0)


def first_kernel(layer_ref, sources_ref, green_ref, src_ref, outs_ref, piece_ref, raw_ref, mats_ref, left_ref, raw_sem, sems):
    nf, nb, nk = green_ref.shape[1:4]
    layer = layer_ref[0]
    way = (layer != 0).astype(jnp.int32)
    active = (layer == 0) | (layer == LAYERS - 1)
    raw_copy = pltpu.make_async_copy(sources_ref, raw_ref, raw_sem)
    raw_copy.start()

    half = nb // 2

    def chunk(f, b):
        at = pl.ds(b, half)
        return pltpu.make_async_copy(green_ref.at[way, f, at], mats_ref.at[f, at], sems.at[f, b // half])

    @pl.when(active)
    def _():
        for f in range(nf):
            for b in range(0, nb, half):
                chunk(f, b).start()

    raw_copy.wait()
    for w in range(2):
        for c in range(2):
            for f in range(nf):
                for b in range(nb):
                    at = (c * nf + f) * nb + b
                    src_ref[w, at : at + 1, :] = raw_ref[w, c, f : f + 1, b * 128 : (b + 1) * 128]

    @pl.when(active)
    def _():
        left_ref[...] = jnp.zeros_like(left_ref)

        def weights(left, f, b):
            if b % half == 0:
                chunk(f, b).wait()
            mats = [jnp.concatenate([mats_ref[f, b + i, k, c] for k in range(nk) for c in range(2)], axis=1) for i in range(2)]
            return lax.dot_general(left, jnp.concatenate(mats, axis=0), (((1,), (1,)), ((), ())), preferred_element_type=F32)

        multiply(left_ref, way, (nf, nb, nk), weights, src_ref, outs_ref, piece_ref)


def first(layer, sources, green):
    nf, nb, nk = green.shape[1:4]
    rows = 2 * nf * nb
    vmem, hbm = pl.BlockSpec(memory_space=pltpu.VMEM), pl.BlockSpec(memory_space=pltpu.HBM)
    return pl.pallas_call(
        first_kernel,
        out_shape=(
            jax.ShapeDtypeStruct((2, rows, 128), F32),
            jax.ShapeDtypeStruct((2, rows, 128), F32),
            jax.ShapeDtypeStruct((rows, 128), BF),
        ),
        in_specs=[pl.BlockSpec(memory_space=pltpu.SMEM), hbm, hbm],
        out_specs=(vmem, vmem, vmem),
        scratch_shapes=[
            pltpu.VMEM(sources.shape, F32),
            pltpu.VMEM(green.shape[1:], BF),
            pltpu.VMEM((nf, 2, nb, 2 * nk * 128), BF),
            pltpu.SemaphoreType.DMA,
            pltpu.SemaphoreType.DMA((nf, 2)),
        ],
        compiler_params=pltpu.CompilerParams(vmem_limit_bytes=12 * 2**20),
        name="first_apply",
    )(layer, sources, green)


def turn_kernel(_, __, green_ref, turned_ref, token_ref, stage_ref, sems):
    nf, nb, nk = green_ref.shape[1:4]
    slots, group = stage_ref.shape[:2]
    per = nb // group
    total = green_ref.shape[0] * nf * per
    token_ref[...] = jnp.zeros_like(token_ref)

    def where(i):
        return i // (nf * per), i // per % nf, i % per * group

    def fetch(i, slot):
        way, f, b = where(i)
        return pltpu.make_async_copy(green_ref.at[way, f, pl.ds(b, group)], stage_ref.at[slot], sems.at[slot])

    for slot in range(slots):
        fetch(slot, slot).start()

    def some(n, carry):
        for slot in range(slots):
            i = n * slots + slot
            fetch(i, slot).wait()
            way, f, b = where(i)
            for g in range(group):
                for k in range(nk):
                    for c in range(2):
                        turned_ref[way, f, b + g, k, c] = stage_ref[slot, g, k, c].T

            @pl.when(i + slots < total)
            def _():
                fetch(i + slots, slot).start()

        return carry

    lax.fori_loop(0, total // slots, some, 0)


def turn(piece, sel, green):
    vmem, hbm = pl.BlockSpec(memory_space=pltpu.VMEM), pl.BlockSpec(memory_space=pltpu.HBM)
    return pl.pallas_call(
        turn_kernel,
        out_shape=(pltpu.VMEM(green.shape, BF), jax.ShapeDtypeStruct((16, 128), BF)),
        in_specs=[vmem, vmem, hbm],
        out_specs=(vmem, vmem),
        scratch_shapes=[pltpu.VMEM((4, 4, *green.shape[3:]), BF), pltpu.SemaphoreType.DMA((4,))],
        compiler_params=pltpu.CompilerParams(vmem_limit_bytes=6 * 2**20),
        cost_estimate=pl.CostEstimate(flops=0, bytes_accessed=16 * 2**20, transcendentals=0),
        name="turn_green",
    )(piece, sel, green)


def apply_kernel(t, layer_ref, sel_ref, src_ref, green_ref, *refs):
    *trace_refs, _, outs_ref, piece_ref, left_ref = refs
    layer = layer_ref[0]
    way = (layer != t).astype(jnp.int32)
    nf, nb, nk = green_ref.shape[1:4]
    part = 2 * nf * nb

    @pl.when((layer == t) | (layer == LAYERS - 1 - t))
    def _():
        columns = []
        for f in range(nf):
            rows = []
            for c in range(2):
                at = (c * nf + f) * nb
                for ref in trace_refs:
                    rows += [ref[p + at : p + at + nb, :] for p in range(0, ref.shape[0], part)]
            columns.append(jnp.concatenate(rows, axis=0))
        picked = jnp.dot(sel_ref[way], jnp.concatenate(columns, axis=1), preferred_element_type=F32).astype(BF)
        for f in range(nf):
            for h in range(2):
                blocks = [picked[(h * 2 * nk + n) * nb : (h * 2 * nk + n + 1) * nb, f * 128 : (f + 1) * 128] for n in range(2 * nk)]
                left_ref[f, h] = jnp.concatenate(blocks, axis=1)

        def weights(left, f, b):
            mats = [jnp.concatenate([green_ref[way, f, b + i, k, c] for k in range(nk) for c in range(2)], axis=0) for i in range(2)]
            return jnp.dot(left, jnp.concatenate(mats, axis=1), preferred_element_type=F32)

        multiply(left_ref, way, (nf, nb, nk), weights, src_ref, outs_ref, piece_ref)


def apply(t, layer, sel, src, green, traces, outs):
    nf, nb, nk = green.shape[1:4]
    vmem = pl.BlockSpec(memory_space=pltpu.VMEM)
    return pl.pallas_call(
        functools.partial(apply_kernel, t),
        out_shape=(jax.ShapeDtypeStruct(outs.shape, F32), jax.ShapeDtypeStruct(outs.shape[1:], BF)),
        in_specs=[pl.BlockSpec(memory_space=pltpu.SMEM)] + [vmem] * (4 + len(traces)),
        out_specs=(vmem, vmem),
        scratch_shapes=[pltpu.VMEM((nf, 2, nb, 2 * nk * 128), BF)],
        input_output_aliases={4 + len(traces): 0},
        compiler_params=pltpu.CompilerParams(vmem_limit_bytes=4 * 2**20),
        name="apply_green",
    )(layer, sel, src, green, *traces, outs)


def selection(index, lat, nb, nk):
    sender = index // nb
    place = (((lat // 2 - sender // 2) % 4) * 2 + (sender % 2 + lat % 2) % 2) * nb + index % nb
    place = place.reshape(2, 2, nb // 2, nk).transpose(0, 1, 3, 2)
    both = lax.broadcasted_iota(jnp.int32, (2, 2, nk, 2, 2, nb // 2), 3) != lax.broadcasted_iota(jnp.int32, (2, 2, nk, 2, 2, nb // 2), 4)
    minus = lax.broadcasted_iota(jnp.int32, (2, 2, nk, 2, 2, nb // 2), 3) > lax.broadcasted_iota(jnp.int32, (2, 2, nk, 2, 2, nb // 2), 4)
    column = place[:, :, :, None, None, :] + jnp.where(both, LAT * nb, 0)
    sign = jnp.where(minus, -1, 1)
    hit = column.reshape(2, -1, 1) == jnp.arange(2 * LAT * nb).reshape(1, 1, -1)
    return jnp.where(hit, sign.reshape(2, -1, 1), 0).astype(BF)


def local(green, block_index, sources):
    nf, nb, nk = green.shape[2:5]
    rows = 2 * nf * nb
    layer, lat = lax.axis_index("layer"), lax.axis_index("lat")
    me = layer.astype(jnp.int32).reshape(1)
    green = pltpu.with_memory_space_constraint(green.reshape(green.shape[1:]), pltpu.HBM)
    raw = pltpu.with_memory_space_constraint(sources.reshape(sources.shape[1:]), pltpu.HBM)
    src, outs, piece = first(me, raw, green)
    sel = selection(block_index[0], lat, nb, nk)
    plan = successors()
    for t in range(LAYERS - 1):
        got = [lax.ppermute(piece, AXES, shift_pairs(plan[t], t, flip)) for flip in (1, 0)]
        pair = jnp.pad(got[1], ((0, rows), (0, 0))) + jnp.pad(got[0], ((rows, 0), (0, 0)))
        if t == 0:
            turned, token = turn(piece, sel, green)
            pair = pair + jnp.tile(token, (pair.shape[0] // token.shape[0], 1))
        far = {k: lax.ppermute(pair, "lat", [(j, (j + 2 * k) % LAT) for j in range(LAT)]) for k in (2, 1, 3)}
        outs, piece = apply(t + 1, me, sel, src, turned, (pair, far[1], far[2], far[3]), outs)
    return outs[0].reshape(1, 2, nf, nb * 128), outs[1].reshape(1, 2, nf, nb * 128)


def solution(mesh):
    placed = (
        P("layer", None, None, "lat", None, None, None, None),
        P("layer", None, "lat", None),
        P("layer", None, None, None, "lat"),
    )
    return jax.shard_map(
        local,
        mesh=mesh,
        in_specs=placed,
        out_specs=(P("layer", None, None, "lat"), P("layer", None, None, "lat")),
        check_vma=False,
    )
```

```python
import functools

import jax
import jax.numpy as jnp
from jax import lax
from jax.experimental import pallas as pl
from jax.experimental.pallas import tpu as pltpu
from jax.sharding import PartitionSpec as P


LAYERS = 16
LAT = 8
AXES = ("layer", "lat")
BF = jnp.bfloat16
F32 = jnp.float32


PLAN = [
    [1, 0, 4, 12, 13, 2, 9, 8, 5, 10, 6, 7, 3, 11, 15, 14],
    [14, 2, 3, 6, 0, 4, 7, 11, 5, 8, 15, 10, 9, 12, 13, 1],
    [1, 0, 3, 2, 5, 4, 7, 6, 9, 13, 11, 10, 8, 12, 15, 14],
    [1, 0, 3, 4, 5, 6, 10, 2, 13, 8, 7, 9, 11, 12, 15, 14],
    [1, 0, 3, 14, 5, 4, 7, 6, 9, 8, 11, 10, 13, 12, 15, 2],
    [1, 0, 3, 2, 5, 6, 7, 11, 4, 8, 9, 10, 13, 12, 15, 14],
    [1, 13, 3, 2, 5, 4, 7, 6, 9, 8, 11, 10, 0, 12, 15, 14],
    [12, 4, 1, 2, 10, 6, 9, 8, 7, 5, 15, 3, 14, 0, 11, 13],
    [1, 3, 15, 2, 5, 4, 7, 6, 9, 8, 11, 14, 0, 12, 10, 13],
    [1, 0, 3, 15, 12, 4, 5, 6, 9, 10, 7, 8, 13, 14, 2, 11],
    [12, 0, 3, 2, 5, 4, 7, 6, 9, 8, 11, 10, 13, 1, 15, 14],
    [13, 5, 14, 2, 3, 4, 7, 6, 9, 8, 11, 12, 0, 1, 15, 10],
    [1, 6, 3, 2, 0, 4, 7, 9, 10, 5, 11, 8, 13, 12, 15, 14],
    [4, 0, 1, 13, 7, 10, 3, 5, 12, 11, 9, 8, 6, 14, 15, 2],
    [1, 0, 4, 9, 11, 8, 13, 2, 7, 10, 12, 6, 5, 3, 15, 14],
]


def shift_pairs(succ, t, flip):
    live = {(t, t + 1), (LAYERS - 1 - t, LAYERS - 2 - t)}
    return sorted(
        (a * LAT + j, b * LAT + ((j ^ flip) if (a, b) in live else j))
        for a, b in succ.items()
        for j in range(LAT)
    )


def multiply(left_ref, way, sizes, weights, src_ref, outs_ref, piece_ref):
    nf, nb, nk = sizes
    half = nb // 2
    rows = lax.broadcasted_iota(jnp.int32, (nb, 128), 0) % half

    def one(n, carry):
        f, h = n // 2, n % 2
        left = left_ref[f, h]
        acc = jnp.zeros((nb, 128), F32)
        for b in range(0, half, 2):
            out = weights(left, f, h, b)
            acc = jnp.where(rows == b, out[:, :128], jnp.where(rows == b + 1, out[:, 128:], acc))
        for c in range(2):
            at = pl.ds(pl.multiple_of((c * nf + f) * nb + h * half, half), half)
            outs_ref[way, at, :] = acc[c * half : (c + 1) * half] + src_ref[way, at, :]
        return carry

    lax.fori_loop(0, 2 * nf, one, 0)
    piece_ref[...] = outs_ref[way].astype(BF)


def first_kernel(layer_ref, sources_ref, green_ref, src_ref, outs_ref, piece_ref, raw_ref, mats_ref, left_ref, raw_sem, sems):
    nf, nb, nk = green_ref.shape[1:4]
    layer = layer_ref[0]
    way = (layer != 0).astype(jnp.int32)
    active = (layer == 0) | (layer == LAYERS - 1)
    raw_copy = pltpu.make_async_copy(sources_ref, raw_ref, raw_sem)
    raw_copy.start()

    half = nb // 2

    def chunk(f, h):
        at = pl.ds(h * half, half)
        return pltpu.make_async_copy(green_ref.at[way, f, at], mats_ref.at[f, at], sems.at[f, h])

    @pl.when(active)
    def _():
        for f in range(nf):
            for h in range(2):
                chunk(f, h).start()

    raw_copy.wait()
    for w in range(2):
        for c in range(2):
            for f in range(nf):
                for b in range(nb):
                    at = (c * nf + f) * nb + b
                    src_ref[w, at : at + 1, :] = raw_ref[w, c, f : f + 1, b * 128 : (b + 1) * 128]

    @pl.when(active)
    def _():
        left_ref[...] = jnp.zeros_like(left_ref)

        def weights(left, f, h, b):
            if b == 0:
                chunk(f, h).wait()
            mats = [jnp.concatenate([mats_ref[f, h * half + b + i, k, c] for k in range(nk) for c in range(2)], axis=1) for i in range(2)]
            return lax.dot_general(left, jnp.concatenate(mats, axis=0), (((1,), (1,)), ((), ())), preferred_element_type=F32)

        multiply(left_ref, way, (nf, nb, nk), weights, src_ref, outs_ref, piece_ref)


def first(layer, sources, green):
    nf, nb, nk = green.shape[1:4]
    rows = 2 * nf * nb
    vmem, hbm = pl.BlockSpec(memory_space=pltpu.VMEM), pl.BlockSpec(memory_space=pltpu.HBM)
    return pl.pallas_call(
        first_kernel,
        out_shape=(
            jax.ShapeDtypeStruct((2, rows, 128), F32),
            jax.ShapeDtypeStruct((2, rows, 128), F32),
            jax.ShapeDtypeStruct((rows, 128), BF),
        ),
        in_specs=[pl.BlockSpec(memory_space=pltpu.SMEM), hbm, hbm],
        out_specs=(vmem, vmem, vmem),
        scratch_shapes=[
            pltpu.VMEM(sources.shape, F32),
            pltpu.VMEM(green.shape[1:], BF),
            pltpu.VMEM((nf, 2, nb, 2 * nk * 128), BF),
            pltpu.SemaphoreType.DMA,
            pltpu.SemaphoreType.DMA((nf, 2)),
        ],
        compiler_params=pltpu.CompilerParams(vmem_limit_bytes=12 * 2**20),
        name="first_apply",
    )(layer, sources, green)


def turn_kernel(_, __, green_ref, turned_ref, token_ref, stage_ref, sems):
    nf, nb, nk = green_ref.shape[1:4]
    slots, group = stage_ref.shape[:2]
    per = nb // group
    total = green_ref.shape[0] * nf * per
    token_ref[...] = jnp.zeros_like(token_ref)

    def where(i):
        return i // (nf * per), i // per % nf, i % per * group

    def fetch(i, slot):
        way, f, b = where(i)
        return pltpu.make_async_copy(green_ref.at[way, f, pl.ds(b, group)], stage_ref.at[slot], sems.at[slot])

    for slot in range(slots):
        fetch(slot, slot).start()

    def some(n, carry):
        for slot in range(slots):
            i = n * slots + slot
            fetch(i, slot).wait()
            way, f, b = where(i)
            for g in range(group):
                for k in range(nk):
                    for c in range(2):
                        turned_ref[way, f, b + g, k, c] = stage_ref[slot, g, k, c].T

            @pl.when(i + slots < total)
            def _():
                fetch(i + slots, slot).start()

        return carry

    lax.fori_loop(0, total // slots, some, 0)


def turn(piece, sel, green):
    vmem, hbm = pl.BlockSpec(memory_space=pltpu.VMEM), pl.BlockSpec(memory_space=pltpu.HBM)
    return pl.pallas_call(
        turn_kernel,
        out_shape=(pltpu.VMEM(green.shape, BF), jax.ShapeDtypeStruct((16, 128), BF)),
        in_specs=[vmem, vmem, hbm],
        out_specs=(vmem, vmem),
        scratch_shapes=[pltpu.VMEM((4, 4, *green.shape[3:]), BF), pltpu.SemaphoreType.DMA((4,))],
        compiler_params=pltpu.CompilerParams(vmem_limit_bytes=6 * 2**20),
        cost_estimate=pl.CostEstimate(flops=0, bytes_accessed=16 * 2**20, transcendentals=0),
        name="turn_green",
    )(piece, sel, green)


def apply_kernel(t, layer_ref, sel_ref, src_ref, green_ref, *refs):
    *trace_refs, _, outs_ref, piece_ref, left_ref = refs
    layer = layer_ref[0]
    way = (layer != t).astype(jnp.int32)
    nf, nb, nk = green_ref.shape[1:4]
    part = 2 * nf * nb

    @pl.when((layer == t) | (layer == LAYERS - 1 - t))
    def _():
        columns = []
        for f in range(nf):
            rows = []
            for c in range(2):
                at = (c * nf + f) * nb
                for ref in trace_refs:
                    rows += [ref[p + at : p + at + nb, :] for p in range(0, ref.shape[0], part)]
            columns.append(jnp.concatenate(rows, axis=0))
        picked = jnp.dot(sel_ref[way], jnp.concatenate(columns, axis=1), preferred_element_type=F32).astype(BF)
        for f in range(nf):
            for h in range(2):
                blocks = [picked[(h * 2 * nk + n) * nb : (h * 2 * nk + n + 1) * nb, f * 128 : (f + 1) * 128] for n in range(2 * nk)]
                left_ref[f, h] = jnp.concatenate(blocks, axis=1)

        def weights(left, f, h, b):
            mats = [jnp.concatenate([green_ref[way, f, h * (nb // 2) + b + i, k, c] for k in range(nk) for c in range(2)], axis=0) for i in range(2)]
            return jnp.dot(left, jnp.concatenate(mats, axis=1), preferred_element_type=F32)

        multiply(left_ref, way, (nf, nb, nk), weights, src_ref, outs_ref, piece_ref)


def apply(t, layer, sel, src, green, traces, outs):
    nf, nb, nk = green.shape[1:4]
    vmem = pl.BlockSpec(memory_space=pltpu.VMEM)
    return pl.pallas_call(
        functools.partial(apply_kernel, t),
        out_shape=(jax.ShapeDtypeStruct(outs.shape, F32), jax.ShapeDtypeStruct(outs.shape[1:], BF)),
        in_specs=[pl.BlockSpec(memory_space=pltpu.SMEM)] + [vmem] * (4 + len(traces)),
        out_specs=(vmem, vmem),
        scratch_shapes=[pltpu.VMEM((nf, 2, nb, 2 * nk * 128), BF)],
        input_output_aliases={4 + len(traces): 0},
        compiler_params=pltpu.CompilerParams(vmem_limit_bytes=4 * 2**20),
        name="apply_green",
    )(layer, sel, src, green, *traces, outs)


def selection(index, lat, nb, nk):
    sender = index // nb
    place = (((lat // 2 - sender // 2) % 4) * 2 + (sender % 2 + lat % 2) % 2) * nb + index % nb
    place = place.reshape(2, 2, nb // 2, nk).transpose(0, 1, 3, 2)
    both = lax.broadcasted_iota(jnp.int32, (2, 2, nk, 2, 2, nb // 2), 3) != lax.broadcasted_iota(jnp.int32, (2, 2, nk, 2, 2, nb // 2), 4)
    minus = lax.broadcasted_iota(jnp.int32, (2, 2, nk, 2, 2, nb // 2), 3) > lax.broadcasted_iota(jnp.int32, (2, 2, nk, 2, 2, nb // 2), 4)
    column = place[:, :, :, None, None, :] + jnp.where(both, LAT * nb, 0)
    sign = jnp.where(minus, -1, 1)
    hit = column.reshape(2, -1, 1) == jnp.arange(2 * LAT * nb).reshape(1, 1, -1)
    return jnp.where(hit, sign.reshape(2, -1, 1), 0).astype(BF)


def local(green, block_index, sources):
    nf, nb, nk = green.shape[2:5]
    rows = 2 * nf * nb
    layer, lat = lax.axis_index("layer"), lax.axis_index("lat")
    me = layer.astype(jnp.int32).reshape(1)
    green = pltpu.with_memory_space_constraint(green.reshape(green.shape[1:]), pltpu.HBM)
    raw = pltpu.with_memory_space_constraint(sources.reshape(sources.shape[1:]), pltpu.HBM)
    src, outs, piece = first(me, raw, green)
    sel = selection(block_index[0], lat, nb, nk)
    plan = [dict(enumerate(row)) for row in PLAN]
    for t in range(LAYERS - 1):
        got = [lax.ppermute(piece, AXES, shift_pairs(plan[t], t, flip)) for flip in (1, 0)]
        pair = jnp.pad(got[1], ((0, rows), (0, 0))) + jnp.pad(got[0], ((rows, 0), (0, 0)))
        if t == 0:
            turned, token = turn(piece, sel, green)
            pair = pair + jnp.tile(token, (pair.shape[0] // token.shape[0], 1))
        far = {k: lax.ppermute(pair, "lat", [(j, (j + 2 * k) % LAT) for j in range(LAT)]) for k in (2, 1, 3)}
        outs, piece = apply(t + 1, me, sel, src, turned, (pair, far[1], far[2], far[3]), outs)
    return outs[0].reshape(1, 2, nf, nb * 128), outs[1].reshape(1, 2, nf, nb * 128)


def solution(mesh):
    placed = (
        P("layer", None, None, "lat", None, None, None, None),
        P("layer", None, "lat", None),
        P("layer", None, None, None, "lat"),
    )
    return jax.shard_map(
        local,
        mesh=mesh,
        in_specs=placed,
        out_specs=(P("layer", None, None, "lat"), P("layer", None, None, "lat")),
        check_vma=False,
    )
```

```python
import functools

import jax
import jax.numpy as jnp
from jax import lax
from jax.experimental import pallas as pl
from jax.experimental.pallas import tpu as pltpu
from jax.sharding import PartitionSpec as P


LAYERS = 16
LAT = 8
AXES = ("layer", "lat")
BF = jnp.bfloat16
F32 = jnp.float32


PLAN = [
    [1, 0, 4, 12, 13, 2, 9, 8, 5, 10, 6, 7, 3, 11, 15, 14],
    [14, 2, 3, 6, 0, 4, 7, 11, 5, 8, 15, 10, 9, 12, 13, 1],
    [1, 0, 3, 2, 5, 4, 7, 6, 9, 13, 11, 10, 8, 12, 15, 14],
    [1, 0, 3, 4, 5, 6, 10, 2, 13, 8, 7, 9, 11, 12, 15, 14],
    [1, 0, 3, 14, 5, 4, 7, 6, 9, 8, 11, 10, 13, 12, 15, 2],
    [1, 0, 3, 2, 5, 6, 7, 11, 4, 8, 9, 10, 13, 12, 15, 14],
    [1, 13, 3, 2, 5, 4, 7, 6, 9, 8, 11, 10, 0, 12, 15, 14],
    [12, 4, 1, 2, 10, 6, 9, 8, 7, 5, 15, 3, 14, 0, 11, 13],
    [1, 3, 15, 2, 5, 4, 7, 6, 9, 8, 11, 14, 0, 12, 10, 13],
    [1, 0, 3, 15, 12, 4, 5, 6, 9, 10, 7, 8, 13, 14, 2, 11],
    [12, 0, 3, 2, 5, 4, 7, 6, 9, 8, 11, 10, 13, 1, 15, 14],
    [13, 5, 14, 2, 3, 4, 7, 6, 9, 8, 11, 12, 0, 1, 15, 10],
    [1, 6, 3, 2, 0, 4, 7, 9, 10, 5, 11, 8, 13, 12, 15, 14],
    [4, 0, 1, 13, 7, 10, 3, 5, 12, 11, 9, 8, 6, 14, 15, 2],
    [1, 0, 4, 9, 11, 8, 13, 2, 7, 10, 12, 6, 5, 3, 15, 14],
]


def shift_pairs(succ, t, flip):
    live = {(t, t + 1), (LAYERS - 1 - t, LAYERS - 2 - t)}
    return sorted(
        (a * LAT + j, b * LAT + ((j ^ flip) if (a, b) in live else j))
        for a, b in succ.items()
        for j in range(LAT)
    )


def multiply(left_ref, way, sizes, weights, src_ref, outs_ref, piece_ref):
    nf, nb, nk = sizes
    half = nb // 2
    rows = lax.broadcasted_iota(jnp.int32, (nb, 128), 0) % half

    def one(n, carry):
        f, h = n // 2, n % 2
        left = left_ref[f, h]
        acc = jnp.zeros((nb, 128), F32)
        for b in range(0, half, 2):
            out = weights(left, f, h, b)
            acc = jnp.where(rows == b, out[:, :128], jnp.where(rows == b + 1, out[:, 128:], acc))
        for c in range(2):
            at = pl.ds(pl.multiple_of((c * nf + f) * nb + h * half, half), half)
            outs_ref[way, at, :] = acc[c * half : (c + 1) * half] + src_ref[way, at, :]
        return carry

    lax.fori_loop(0, 2 * nf, one, 0)
    piece_ref[...] = outs_ref[way].astype(BF)


def first_kernel(layer_ref, sources_ref, green_ref, src_ref, outs_ref, piece_ref, raw_ref, mats_ref, left_ref, raw_sem, sems):
    nf, nb, nk = green_ref.shape[1:4]
    layer = layer_ref[0]
    way = (layer != 0).astype(jnp.int32)
    active = (layer == 0) | (layer == LAYERS - 1)
    raw_copy = pltpu.make_async_copy(sources_ref, raw_ref, raw_sem)
    raw_copy.start()

    half = nb // 2

    def chunk(f, h):
        at = pl.ds(h * half, half)
        return pltpu.make_async_copy(green_ref.at[way, f, at], mats_ref.at[f, at], sems.at[f, h])

    @pl.when(active)
    def _():
        for f in range(nf):
            for h in range(2):
                chunk(f, h).start()

    raw_copy.wait()
    for w in range(2):
        for c in range(2):
            for f in range(nf):
                for b in range(nb):
                    at = (c * nf + f) * nb + b
                    src_ref[w, at : at + 1, :] = raw_ref[w, c, f : f + 1, b * 128 : (b + 1) * 128]

    @pl.when(active)
    def _():
        left_ref[...] = jnp.zeros_like(left_ref)

        def weights(left, f, h, b):
            if b == 0:
                chunk(f, h).wait()
            mats = [jnp.concatenate([mats_ref[f, h * half + b + i, k, c] for k in range(nk) for c in range(2)], axis=1) for i in range(2)]
            return lax.dot_general(left, jnp.concatenate(mats, axis=0), (((1,), (1,)), ((), ())), preferred_element_type=F32)

        multiply(left_ref, way, (nf, nb, nk), weights, src_ref, outs_ref, piece_ref)


def first(layer, sources, green):
    nf, nb, nk = green.shape[1:4]
    rows = 2 * nf * nb
    vmem, hbm = pl.BlockSpec(memory_space=pltpu.VMEM), pl.BlockSpec(memory_space=pltpu.HBM)
    return pl.pallas_call(
        first_kernel,
        out_shape=(
            jax.ShapeDtypeStruct((2, rows, 128), F32),
            jax.ShapeDtypeStruct((2, rows, 128), F32),
            jax.ShapeDtypeStruct((rows, 128), BF),
        ),
        in_specs=[pl.BlockSpec(memory_space=pltpu.SMEM), hbm, hbm],
        out_specs=(vmem, vmem, vmem),
        scratch_shapes=[
            pltpu.VMEM(sources.shape, F32),
            pltpu.VMEM(green.shape[1:], BF),
            pltpu.VMEM((nf, 2, nb, 2 * nk * 128), BF),
            pltpu.SemaphoreType.DMA,
            pltpu.SemaphoreType.DMA((nf, 2)),
        ],
        compiler_params=pltpu.CompilerParams(vmem_limit_bytes=12 * 2**20),
        name="first_apply",
    )(layer, sources, green)


def turn_kernel(_, __, green_ref, turned_ref, token_ref, stage_ref, sems):
    nf, nb, nk = green_ref.shape[1:4]
    slots, group = stage_ref.shape[:2]
    per = nb // group
    total = green_ref.shape[0] * nf * per
    token_ref[...] = jnp.zeros_like(token_ref)

    def where(i):
        return i // (nf * per), i // per % nf, i % per * group

    def fetch(i, slot):
        way, f, b = where(i)
        return pltpu.make_async_copy(green_ref.at[way, f, pl.ds(b, group)], stage_ref.at[slot], sems.at[slot])

    for slot in range(slots):
        fetch(slot, slot).start()

    def some(n, carry):
        for slot in range(slots):
            i = n * slots + slot
            fetch(i, slot).wait()
            way, f, b = where(i)
            for g in range(group):
                for k in range(nk):
                    for c in range(2):
                        turned_ref[way, f, b + g, k, c] = stage_ref[slot, g, k, c].T

            @pl.when(i + slots < total)
            def _():
                fetch(i + slots, slot).start()

        return carry

    lax.fori_loop(0, total // slots, some, 0)


def turn(piece, sel, green):
    vmem, hbm = pl.BlockSpec(memory_space=pltpu.VMEM), pl.BlockSpec(memory_space=pltpu.HBM)
    return pl.pallas_call(
        turn_kernel,
        out_shape=(pltpu.VMEM(green.shape, BF), jax.ShapeDtypeStruct((16, 128), BF)),
        in_specs=[vmem, vmem, hbm],
        out_specs=(vmem, vmem),
        scratch_shapes=[pltpu.VMEM((4, 4, *green.shape[3:]), BF), pltpu.SemaphoreType.DMA((4,))],
        compiler_params=pltpu.CompilerParams(vmem_limit_bytes=6 * 2**20),
        cost_estimate=pl.CostEstimate(flops=0, bytes_accessed=16 * 2**20, transcendentals=0),
        name="turn_green",
    )(piece, sel, green)


def apply_kernel(t, layer_ref, sel_ref, src_ref, green_ref, *refs):
    *trace_refs, _, outs_ref, piece_ref, left_ref = refs
    layer = layer_ref[0]
    way = (layer != t).astype(jnp.int32)
    nf, nb, nk = green_ref.shape[1:4]
    part = 2 * nf * nb

    @pl.when((layer == t) | (layer == LAYERS - 1 - t))
    def _():
        columns = []
        for f in range(nf):
            rows = []
            for c in range(2):
                at = (c * nf + f) * nb
                for ref in trace_refs:
                    rows += [ref[p + at : p + at + nb, :] for p in range(0, ref.shape[0], part)]
            columns.append(jnp.concatenate(rows, axis=0))
        picked = jnp.dot(sel_ref[way], jnp.concatenate(columns, axis=1), preferred_element_type=F32).astype(BF)
        for f in range(nf):
            for h in range(2):
                blocks = [picked[(h * 2 * nk + n) * nb : (h * 2 * nk + n + 1) * nb, f * 128 : (f + 1) * 128] for n in range(2 * nk)]
                left_ref[f, h] = jnp.concatenate(blocks, axis=1)

        def weights(left, f, h, b):
            mats = [jnp.concatenate([green_ref[way, f, h * (nb // 2) + b + i, k, c] for k in range(nk) for c in range(2)], axis=0) for i in range(2)]
            return jnp.dot(left, jnp.concatenate(mats, axis=1), preferred_element_type=F32)

        multiply(left_ref, way, (nf, nb, nk), weights, src_ref, outs_ref, piece_ref)


def apply(t, layer, sel, src, green, traces, outs):
    nf, nb, nk = green.shape[1:4]
    vmem = pl.BlockSpec(memory_space=pltpu.VMEM)
    return pl.pallas_call(
        functools.partial(apply_kernel, t),
        out_shape=(jax.ShapeDtypeStruct(outs.shape, F32), jax.ShapeDtypeStruct(outs.shape[1:], BF)),
        in_specs=[pl.BlockSpec(memory_space=pltpu.SMEM)] + [vmem] * (4 + len(traces)),
        out_specs=(vmem, vmem),
        scratch_shapes=[pltpu.VMEM((nf, 2, nb, 2 * nk * 128), BF)],
        input_output_aliases={4 + len(traces): 0},
        compiler_params=pltpu.CompilerParams(vmem_limit_bytes=4 * 2**20),
        name="apply_green",
    )(layer, sel, src, green, *traces, outs)


def selection(index, lat, nb, nk):
    place = jnp.bitwise_xor(index // nb, lat) * nb + index % nb
    place = place.reshape(2, 2, nb // 2, nk).transpose(0, 1, 3, 2)
    both = lax.broadcasted_iota(jnp.int32, (2, 2, nk, 2, 2, nb // 2), 3) != lax.broadcasted_iota(jnp.int32, (2, 2, nk, 2, 2, nb // 2), 4)
    minus = lax.broadcasted_iota(jnp.int32, (2, 2, nk, 2, 2, nb // 2), 3) > lax.broadcasted_iota(jnp.int32, (2, 2, nk, 2, 2, nb // 2), 4)
    column = place[:, :, :, None, None, :] + jnp.where(both, LAT * nb, 0)
    sign = jnp.where(minus, -1, 1)
    hit = column.reshape(2, -1, 1) == jnp.arange(2 * LAT * nb).reshape(1, 1, -1)
    return jnp.where(hit, sign.reshape(2, -1, 1), 0).astype(BF)


def local(green, block_index, sources):
    nf, nb, nk = green.shape[2:5]
    rows = 2 * nf * nb
    layer, lat = lax.axis_index("layer"), lax.axis_index("lat")
    me = layer.astype(jnp.int32).reshape(1)
    green = pltpu.with_memory_space_constraint(green.reshape(green.shape[1:]), pltpu.HBM)
    raw = pltpu.with_memory_space_constraint(sources.reshape(sources.shape[1:]), pltpu.HBM)
    src, outs, piece = first(me, raw, green)
    sel = selection(block_index[0], lat, nb, nk)
    plan = [dict(enumerate(row)) for row in PLAN]
    for t in range(LAYERS - 1):
        got = [lax.ppermute(piece, AXES, shift_pairs(plan[t], t, flip)) for flip in (1, 0)]
        pair = jnp.pad(got[1], ((0, rows), (0, 0))) + jnp.pad(got[0], ((rows, 0), (0, 0)))
        if t == 0:
            turned, token = turn(piece, sel, green)
            pair = pair + jnp.tile(token, (pair.shape[0] // token.shape[0], 1))
        far = {mask: lax.ppermute(pair, "lat", [(j, j ^ mask) for j in range(LAT)]) for mask in (4, 6, 2)}
        outs, piece = apply(t + 1, me, sel, src, turned, (pair, far[2], far[4], far[6]), outs)
    return outs[0].reshape(1, 2, nf, nb * 128), outs[1].reshape(1, 2, nf, nb * 128)


def solution(mesh):
    placed = (
        P("layer", None, None, "lat", None, None, None, None),
        P("layer", None, "lat", None),
        P("layer", None, None, None, "lat"),
    )
    return jax.shard_map(
        local,
        mesh=mesh,
        in_specs=placed,
        out_specs=(P("layer", None, None, "lat"), P("layer", None, None, "lat")),
        check_vma=False,
    )
```
